1024 devices in a mesh: seq: 128 (over z, x), head: 8 (over y, core).
Axes of the slice: x: 4, y: 4, z: 32, core: 2. Of those that a mesh axis runs over, the one named last changes fastest.
Arguments:
- queries: bfloat16 [16384, 4096], P('seq', 'head'), may hold values from -150 to 150
- neighbours: bfloat16 [128, 128, 8, 448], P(None, 'seq', None, 'head'), may hold values from -6 to 6
- key_weight: bfloat16 [448, 4096], P(None, 'head'), may hold values from -0.25 to 0.25
- value_weight: bfloat16 [448, 4096], P(None, 'head'), may hold values from -0.25 to 0.25
- counts: int32 [256], P('seq'), may hold values from 1 to 4, as said below
- slot_map: int32 [128, 8], P('seq'), may hold values from 0 to 7, each once within a row
- d_attended: bfloat16 [16384, 4096], P('seq', 'head'), may hold values from -6 to 6
Outputs:
- attended: bfloat16 [16384, 4096], P('seq', 'head')
- d_queries: bfloat16 [16384, 4096], P('seq', 'head')
- d_neighbours: bfloat16 [128, 128, 8, 448], P(None, 'seq', None, 'head')
The draws below stay inside these ranges and needn't reach their ends.
Inputs may be any that keep to these rules, and one draw needn't show every extreme that they name: `counts`: every span has at least one neighbour; some span has 4. `slot_map`: each row is a permutation; entry c * 4 + j names the slot that holds neighbour j of local span c, and only entries with j below the span's count are used.
All inputs are finite; a program needn't handle non-finite values.
Results may differ from the reference program's by a relative error of at most 0.03.
Values may be sent and summed in bfloat16 or wider, within the bound.
No kernel may reach another device: no remote copies, remote signals or barrier semaphores. Data moves between devices by JAX's collectives and lax.ppermute only.
A program may use at most 32 MiB of HBM per device.

```python
import jax
import jax.numpy as jnp
from jax import lax

HEADS = 32
HDIM = 128
ENC = 448
SPAN = 64
NB_LEN = 128
MAX_NB = 4
CH_DEV = 2
TOK_DEV = 128
SLOTS = 8
TOKENS = 16384
SPANS = 256
GROUPS = 128
N_SEQ = 128
N_HEAD = 8


def draw_queries(key, part):
    shape = (TOKENS, HEADS * HDIM)
    values = jnp.clip(jax.random.normal(jax.random.fold_in(key, 4), shape, jnp.float32), -6.0, 6.0)
    return values.astype(jnp.bfloat16)


def draw_counts(key, part):
    values = jax.random.randint(jax.random.fold_in(key, 11), (SPANS,), 1, MAX_NB + 1)
    spot = jax.random.randint(jax.random.fold_in(key, 12), (), 0, SPANS)
    values = values.at[spot].set(MAX_NB)
    return values.astype(jnp.int32)


def steps_of(stream_key, shape, pieces, low, high):
    def one(dim, blocks):
        heights = jax.random.uniform(jax.random.fold_in(jax.random.fold_in(stream_key, 6), dim), (blocks,), jnp.float32, low / len(pieces), high / len(pieces))
        return jnp.repeat(jnp.exp(heights), shape[dim] // blocks).reshape((-1,) + (1,) * (len(shape) - dim - 1))

    loudness = one(*pieces[0])
    for cut in pieces[1:]:
        loudness = loudness * one(*cut)
    return loudness


def noise(key, shape, deviation, reach, split=(), kind=jnp.bfloat16):
    array = jax.random.normal(key, shape, jnp.float32) * deviation
    if len(split) > 0:
        array = steps_of(key, shape, split, -0.22, 0.18) * array
    return jnp.clip(array, min=-reach, max=reach).astype(kind)


def setup_inputs(seed: int = 0) -> dict:
    streams_of = jax.random.split(jax.random.key(seed), 8)
    return {
        "queries": draw_queries(jax.random.fold_in(streams_of[7], 71), 0),
        "neighbours": noise(streams_of[1], (GROUPS, NB_LEN, SLOTS, ENC), 1.0, 6.0, ((1, 128), (3, 8))),
        "key_weight": noise(streams_of[2], (ENC, HEADS * HDIM), ENC ** -0.5, 0.25, ((1, 8),)),
        "value_weight": noise(streams_of[3], (ENC, HEADS * HDIM), ENC ** -0.5, 0.25, ((1, 8),)),
        "counts": draw_counts(jax.random.fold_in(streams_of[7], 71), 0),
        "slot_map": jax.vmap(lambda own: jax.random.permutation(own, SLOTS))(jax.random.split(streams_of[5], GROUPS)).reshape((GROUPS, SLOTS)).astype(jnp.int32),
        "d_attended": noise(streams_of[6], (TOKENS, HEADS * HDIM), 1.0, 6.0, ((0, 128), (1, 8))),
    }


def present_table(count_row, slot_row):
    chosen = slot_row.reshape(CH_DEV, MAX_NB)
    ranks = jnp.arange(MAX_NB, dtype=jnp.int32)
    valid = ranks[None, :] < count_row[:, None]
    slot_ids = jnp.arange(SLOTS, dtype=jnp.int32)
    hits = valid[:, :, None] & (chosen[:, :, None] == slot_ids[None, None, :])
    return jnp.any(hits, axis=1)


def attend_group(query_rows, enc_rows, count_row, slot_row, grad_rows, key_weight, value_weight):
    total_rows = NB_LEN * SLOTS
    width = HEADS * HDIM
    highest = lax.Precision.HIGHEST
    flat_rows = enc_rows.reshape(total_rows, ENC)
    keys = jnp.dot(flat_rows, key_weight, preferred_element_type=jnp.float32)
    values = jnp.dot(flat_rows, value_weight, preferred_element_type=jnp.float32).astype(jnp.bfloat16)
    present = present_table(count_row, slot_row)
    allowed = jnp.tile(jnp.repeat(present, SPAN, axis=0), (1, NB_LEN))
    factor = 1.0 / (HDIM ** 0.5)
    query_heads = query_rows.reshape(TOK_DEV, HEADS, HDIM).astype(jnp.float32)
    key_heads = keys.reshape(total_rows, HEADS, HDIM).astype(jnp.float32)
    value_heads = values.reshape(total_rows, HEADS, HDIM).astype(jnp.float32)
    grad_heads = grad_rows.reshape(TOK_DEV, HEADS, HDIM).astype(jnp.float32)
    scores = jnp.einsum("thd,rhd->htr", query_heads, key_heads, precision=highest) * factor
    scores = jnp.where(allowed[None, :, :], scores, -jnp.inf)
    top = jnp.max(scores, axis=-1, keepdims=True)
    expo = jnp.exp(scores - top)
    probs = expo / jnp.sum(expo, axis=-1, keepdims=True)
    probs_b = probs.astype(jnp.bfloat16)
    attended = jnp.einsum("htr,rhd->thd", probs_b.astype(jnp.float32), value_heads)
    attended = attended.astype(jnp.bfloat16).reshape(TOK_DEV, width)
    dprobs = jnp.einsum("thd,rhd->htr", grad_heads, value_heads)
    inner = jnp.sum(probs * dprobs, axis=-1, keepdims=True)
    dscores = (probs * (dprobs - inner)).astype(jnp.bfloat16).astype(jnp.float32)
    d_queries = (jnp.einsum("htr,rhd->thd", dscores, key_heads, precision=highest) * factor).astype(jnp.bfloat16)
    d_keys = (jnp.einsum("htr,thd->rhd", dscores, query_heads) * factor).astype(jnp.bfloat16)
    d_values = jnp.einsum("htr,thd->rhd", probs_b.astype(jnp.float32), grad_heads).astype(jnp.bfloat16)
    local_width = width // N_HEAD
    dk_blocks = d_keys.reshape(total_rows, N_HEAD, local_width).astype(jnp.float32)
    dv_blocks = d_values.reshape(total_rows, N_HEAD, local_width).astype(jnp.float32)
    wk_blocks = key_weight.reshape(ENC, N_HEAD, local_width).astype(jnp.float32)
    wv_blocks = value_weight.reshape(ENC, N_HEAD, local_width).astype(jnp.float32)
    partial_value = jnp.einsum("rjc,ejc->jre", dk_blocks, wk_blocks) + jnp.einsum("rjc,ejc->jre", dv_blocks, wv_blocks)
    partial_value = lax.optimization_barrier(partial_value.astype(jnp.bfloat16)).astype(jnp.float32)
    summed = jnp.sum(partial_value, axis=0).astype(jnp.bfloat16).reshape(NB_LEN, SLOTS, ENC)
    return attended, d_queries.reshape(TOK_DEV, width), summed


def reference(queries, neighbours, key_weight, value_weight, counts, slot_map, d_attended):
    width = HEADS * HDIM
    query_groups = queries.reshape(N_SEQ, TOK_DEV, width)
    grad_groups = d_attended.reshape(N_SEQ, TOK_DEV, width)
    count_groups = counts.reshape(N_SEQ, CH_DEV)

    def one_group(items):
        return attend_group(items[0], items[1], items[2], items[3], items[4], key_weight, value_weight)

    attended, d_queries, d_neighbours = lax.map(one_group, (query_groups, neighbours, count_groups, slot_map, grad_groups))
    return attended.reshape(TOKENS, width), d_queries.reshape(TOKENS, width), d_neighbours
```

```python
import jax
import jax.numpy as jnp
from jax import lax
from jax.experimental import pallas as pl
from jax.experimental.pallas import tpu as pltpu
from jax.sharding import PartitionSpec as P

HDIM = 128
SPAN = 64
NB_LEN = 128
MAX_NB = 4
CH_DEV = 2
SLOTS = 8
LANES = 128
BF = jnp.bfloat16
F32 = jnp.float32
VMEM_LIMIT = 48 * 1024 * 1024


def vmem():
    return pl.BlockSpec(memory_space=pltpu.VMEM)


def smem():
    return pl.BlockSpec(memory_space=pltpu.SMEM)


def to_messages(flat, out_ref):
    blocks = out_ref.shape[1]
    extra = blocks * LANES - flat.shape[0]
    turned = jnp.concatenate([flat, jnp.zeros((extra, flat.shape[1]), flat.dtype)], axis=0).T
    turned = turned.astype(BF)
    for i in range(blocks):
        out_ref[:, i, :] = turned[:, i * LANES : (i + 1) * LANES]


def pack_kernel(flat_ref, out_ref):
    to_messages(flat_ref[...], out_ref)


def unpack_kernel(in_ref, out_ref):
    parts = [in_ref[:, i, :] for i in range(in_ref.shape[1])]
    out_ref[...] = jnp.concatenate(parts, axis=1).T[: out_ref.shape[0]]


def sum_pack_kernel(parts_ref, out_ref):
    total = parts_ref[0].astype(F32)
    for i in range(1, parts_ref.shape[0]):
        total = total + parts_ref[i].astype(F32)
    to_messages(total.astype(BF), out_ref)


def attend_kernel(counts_ref, slots_ref, rows_ref, up_ref, down_ref, q_ref, g_ref, att_ref, dq_ref, part_ref, x_ref, dkv_ref):
    n_head = rows_ref.shape[0]
    chunk = rows_ref.shape[2]
    heads = q_ref.shape[1] // HDIM
    span_rows = MAX_NB * NB_LEN
    factor = 1.0 / HDIM**0.5
    for j in range(SLOTS):
        slot = slots_ref[0, j]
        for b in range(n_head):
            x_ref[b * chunk : (b + 1) * chunk, j * NB_LEN : (j + 1) * NB_LEN] = rows_ref[b, slot]
    lane = lax.broadcasted_iota(jnp.int32, (SPAN, span_rows), 1)
    nt = (((1,), (1,)), ((), ()))
    tn = (((0,), (0,)), ((), ()))
    for h in range(heads):
        lo, hi = h * HDIM, (h + 1) * HDIM
        kv = jnp.dot(up_ref[2 * lo : 2 * hi, :], x_ref[...], preferred_element_type=F32)
        key = kv[:HDIM]
        value = kv[HDIM:].astype(BF)
        key_hi = key.astype(BF)
        key_lo = (key - key_hi.astype(F32)).astype(BF)
        key_two = jnp.concatenate([key_hi, key_lo], axis=0)
        for c in range(CH_DEV):
            tok = slice(c * SPAN, (c + 1) * SPAN)
            own = slice(c * span_rows, (c + 1) * span_rows)
            query = q_ref[tok, lo:hi]
            grad = g_ref[tok, lo:hi]
            k_c = key_two[:, own]
            v_c = value[:, own]
            scores = jnp.dot(jnp.concatenate([query, query], axis=1), k_c, preferred_element_type=F32) * factor
            scores = jnp.where(lane < counts_ref[c] * NB_LEN, scores, -jnp.inf)
            top = jnp.max(scores, axis=1, keepdims=True)
            expo = jnp.exp(scores - top)
            probs = expo * (1.0 / jnp.sum(expo, axis=1, keepdims=True))
            probs_b = probs.astype(BF)
            dprobs = jnp.dot(grad, v_c, preferred_element_type=F32)
            inner = jnp.sum(probs * dprobs, axis=1, keepdims=True)
            dscores = (probs * (dprobs - inner)).astype(BF)
            att = lax.dot_general(probs_b, v_c, nt, preferred_element_type=F32)
            att_ref[tok, lo:hi] = att.astype(BF)
            dq = lax.dot_general(dscores, k_c, nt, preferred_element_type=F32)
            dq_ref[tok, lo:hi] = ((dq[:, :HDIM] + dq[:, HDIM:]) * factor).astype(BF)
            dk = lax.dot_general(query, dscores, tn, preferred_element_type=F32) * factor
            dv = lax.dot_general(grad, probs_b, tn, preferred_element_type=F32)
            dkv_ref[2 * lo : 2 * lo + HDIM, own] = dk.astype(BF)
            dkv_ref[2 * lo + HDIM : 2 * hi, own] = dv.astype(BF)
    part = jnp.dot(down_ref[...], dkv_ref[...], preferred_element_type=F32).astype(BF)
    for j in range(SLOTS):
        slot = slots_ref[0, j]
        for b in range(n_head):
            part_ref[b, slot] = part[b * chunk : (b + 1) * chunk, j * NB_LEN : (j + 1) * NB_LEN]


def params():
    return pltpu.CompilerParams(vmem_limit_bytes=VMEM_LIMIT)


def per_device(queries, neighbours, key_weight, value_weight, counts, slot_map, d_attended):
    n_seq = neighbours.shape[0]
    chunk = neighbours.shape[3]
    enc, width = key_weight.shape
    n_head = enc // chunk
    heads = width // HDIM
    flat = SLOTS * chunk
    blocks = -(-flat // LANES)
    messages = jax.ShapeDtypeStruct((n_seq, blocks, LANES), BF)

    turned = neighbours.transpose(1, 2, 3, 0).reshape(flat, n_seq)
    out = pl.pallas_call(pack_kernel, out_shape=messages, in_specs=[vmem()], out_specs=vmem(), compiler_params=params(), name="pack")(turned)
    arrived = lax.all_to_all(out, "seq", split_axis=0, concat_axis=0, tiled=True)
    both = jnp.stack([key_weight.reshape(enc, heads, HDIM), value_weight.reshape(enc, heads, HDIM)], axis=2)
    down = both.reshape(enc, 2 * width)
    up = down.T
    rows = pl.pallas_call(
        unpack_kernel, out_shape=jax.ShapeDtypeStruct((flat, NB_LEN), BF), in_specs=[vmem()], out_specs=vmem(), compiler_params=params(), name="unpack"
    )(arrived)
    rows = lax.all_gather(rows, "head", axis=0, tiled=True).reshape(n_head, SLOTS, chunk, NB_LEN)
    attended, d_queries, partial_value = pl.pallas_call(
        attend_kernel,
        out_shape=(
            jax.ShapeDtypeStruct(queries.shape, BF),
            jax.ShapeDtypeStruct(queries.shape, BF),
            jax.ShapeDtypeStruct((n_head, SLOTS, chunk, NB_LEN), BF),
        ),
        in_specs=[smem(), smem()] + [vmem()] * 5,
        out_specs=(vmem(), vmem(), vmem()),
        scratch_shapes=[pltpu.VMEM((enc, SLOTS * NB_LEN), BF), pltpu.VMEM((2 * width, SLOTS * NB_LEN), BF)],
        compiler_params=params(),
        name="attend",
    )(counts, slot_map, rows, up, down, queries, d_attended)
    pieces = lax.all_to_all(partial_value.reshape(n_head, flat, NB_LEN), "head", split_axis=0, concat_axis=0, tiled=True)
    back = pl.pallas_call(
        sum_pack_kernel, out_shape=jax.ShapeDtypeStruct((NB_LEN, blocks, LANES), BF), in_specs=[vmem()], out_specs=vmem(), compiler_params=params(), name="sum_pack"
    )(pieces)
    home = lax.all_to_all(back, "seq", split_axis=0, concat_axis=0, tiled=True)
    grad = pl.pallas_call(
        unpack_kernel, out_shape=jax.ShapeDtypeStruct((flat, n_seq), BF), in_specs=[vmem()], out_specs=vmem(), compiler_params=params(), name="unpack_back"
    )(home)
    d_neighbours = grad.reshape(1, SLOTS, chunk, n_seq).transpose(3, 0, 1, 2)
    return (attended, d_queries, d_neighbours)


def solution(mesh):
    in_specs = (
        P("seq", "head"),
        P(None, "seq", None, "head"),
        P(None, "head"),
        P(None, "head"),
        P("seq"),
        P("seq", None),
        P("seq", "head"),
    )
    out_specs = (P("seq", "head"), P("seq", "head"), P(None, "seq", None, "head"))
    return jax.shard_map(
        per_device, mesh=mesh, in_specs=in_specs, out_specs=out_specs, check_vma=False
    )
```

```python
import jax
import jax.numpy as jnp
from jax import lax
from jax.experimental import pallas as pl
from jax.experimental.pallas import tpu as pltpu
from jax.sharding import Mesh, PartitionSpec as P

HDIM = 128
SPAN = 64
NB_LEN = 128
MAX_NB = 4
CH_DEV = 2
SLOTS = 8
LANES = 128
X_CHIPS = 4
CORES = 2
FIRST_IN = 24
FIRST_OUT = 16
BF = jnp.bfloat16
F32 = jnp.float32
VMEM_LIMIT = 48 * 1024 * 1024


def vmem():
    return pl.BlockSpec(memory_space=pltpu.VMEM)


def smem():
    return pl.BlockSpec(memory_space=pltpu.SMEM)


def to_rows(flat):
    extra = -flat.shape[0] % LANES
    return jnp.concatenate([flat, jnp.zeros((extra, flat.shape[1]), flat.dtype)], axis=0).T


def swapped(n, first):
    run = first & -first if first else n
    return [(slice(k ^ first, (k ^ first) + run), slice(k, k + run)) for k in range(0, n, run)]


def scaled(run, by):
    return slice(run.start * by, run.stop * by)


def pack_kernel(flat_ref, out_ref):
    turned = to_rows(flat_ref[...])
    n_x = X_CHIPS
    for src, dst in swapped(out_ref.shape[0] // n_x, FIRST_IN):
        for i in range(out_ref.shape[1]):
            out_ref[scaled(dst, n_x), i, :] = turned[scaled(src, n_x), i * LANES : (i + 1) * LANES]


def unpack_kernel(in_ref, out_ref):
    n_x = X_CHIPS
    runs = swapped(in_ref.shape[0] // n_x, FIRST_OUT)
    parts = [jnp.concatenate([in_ref[scaled(src, n_x), i, :] for src, _ in runs], axis=0) for i in range(in_ref.shape[1])]
    out_ref[...] = jnp.concatenate(parts, axis=1).T[: out_ref.shape[0]]


def spread_kernel(in_ref, out_ref):
    for x in range(out_ref.shape[0]):
        own = in_ref[:, x]
        for y in range(out_ref.shape[1]):
            out_ref[x, y] = own


def turn_kernel(in_ref, out_ref):
    n_x, n_y, _, blocks, _ = in_ref.shape
    for y in range(n_y):
        rows = [jnp.concatenate([in_ref[x, y, :, i, :] for x in range(n_x)], axis=0) for i in range(blocks)]
        out_ref[y] = jnp.concatenate(rows, axis=1).T[: out_ref.shape[1]]


def join_kernel(keep_ref, got_ref, out_ref):
    n_x, n_y, n_z, blocks, _ = out_ref.shape
    for y in range(n_y):
        turned = to_rows((keep_ref[y].astype(F32) + got_ref[y].astype(F32)).astype(BF))
        for x in range(n_x):
            for i in range(blocks):
                out_ref[x, y, :, i, :] = turned[x * n_z : (x + 1) * n_z, i * LANES : (i + 1) * LANES]


def sum_kernel(in_ref, out_ref):
    n_x, n_y = in_ref.shape[:2]
    for x in range(n_x):
        total = in_ref[x, 0].astype(F32)
        for y in range(1, n_y):
            total = total + in_ref[x, y].astype(F32)
        total = total.astype(BF)
        for src, dst in swapped(out_ref.shape[0], FIRST_IN ^ FIRST_OUT):
            out_ref[dst, x] = total[src]


def attend_kernel(
    counts_ref, slots_ref, core_ref, rows_ref, wk_ref, wv_ref, q_ref, g_ref, att_ref, dq_ref, keep_ref, send_ref, x_ref, dk_ref, dv_ref, part_ref
):
    n_core, n_y, _, chunk, _ = rows_ref.shape
    heads = q_ref.shape[1] // HDIM
    span_rows = MAX_NB * NB_LEN
    factor = 1.0 / HDIM**0.5
    for j in range(SLOTS):
        slot = slots_ref[0, j]
        for b in range(n_core * n_y):
            x_ref[b * chunk : (b + 1) * chunk, j * NB_LEN : (j + 1) * NB_LEN] = rows_ref[b % n_core, b // n_core, slot]
    lane = lax.broadcasted_iota(jnp.int32, (SPAN, span_rows), 1)
    nt = (((1,), (1,)), ((), ()))
    tn = (((0,), (0,)), ((), ()))
    for h in range(heads):
        lo, hi = h * HDIM, (h + 1) * HDIM
        key = lax.dot_general(wk_ref[:, lo:hi], x_ref[...], tn, preferred_element_type=F32)
        value = lax.dot_general(wv_ref[:, lo:hi], x_ref[...], tn, preferred_element_type=F32).astype(BF)
        key_hi = key.astype(BF)
        key_lo = (key - key_hi.astype(F32)).astype(BF)
        key_two = jnp.concatenate([key_hi, key_lo], axis=0)
        for c in range(CH_DEV):
            tok = slice(c * SPAN, (c + 1) * SPAN)
            own = slice(c * span_rows, (c + 1) * span_rows)
            query = q_ref[tok, lo:hi]
            grad = g_ref[tok, lo:hi]
            k_c = key_two[:, own]
            v_c = value[:, own]
            scores = jnp.dot(jnp.concatenate([query, query], axis=1), k_c, preferred_element_type=F32) * factor
            scores = jnp.where(lane < counts_ref[c] * NB_LEN, scores, -jnp.inf)
            top = jnp.max(scores, axis=1, keepdims=True)
            expo = jnp.exp(scores - top)
            probs = expo * (1.0 / jnp.sum(expo, axis=1, keepdims=True))
            probs_b = probs.astype(BF)
            dprobs = jnp.dot(grad, v_c, preferred_element_type=F32)
            inner = jnp.sum(probs * dprobs, axis=1, keepdims=True)
            dscores = (probs * (dprobs - inner)).astype(BF)
            att = lax.dot_general(probs_b, v_c, nt, preferred_element_type=F32)
            att_ref[tok, lo:hi] = att.astype(BF)
            dq = lax.dot_general(dscores, k_c, nt, preferred_element_type=F32)
            dq_ref[tok, lo:hi] = ((dq[:, :HDIM] + dq[:, HDIM:]) * factor).astype(BF)
            dk = lax.dot_general(query, dscores, tn, preferred_element_type=F32) * factor
            dv = lax.dot_general(grad, probs_b, tn, preferred_element_type=F32)
            dk_ref[lo:hi, own] = dk.astype(BF)
            dv_ref[lo:hi, own] = dv.astype(BF)
    part = jnp.dot(wk_ref[...], dk_ref[...], preferred_element_type=F32)
    part = (part + jnp.dot(wv_ref[...], dv_ref[...], preferred_element_type=F32)).astype(BF)
    for b in range(n_core * n_y):
        part_ref[b] = part[b * chunk : (b + 1) * chunk]
    core = core_ref[0]
    for j in range(SLOTS):
        slot = slots_ref[0, j]
        for y in range(n_y):
            keep_ref[y, slot] = part_ref[y * n_core + core, :, j * NB_LEN : (j + 1) * NB_LEN]
            send_ref[y, slot] = part_ref[y * n_core + 1 - core, :, j * NB_LEN : (j + 1) * NB_LEN]


def call(kernel, outs, n_in, name, small=0, scratch=()):
    one = isinstance(outs, jax.ShapeDtypeStruct)
    return pl.pallas_call(
        kernel,
        out_shape=outs,
        in_specs=[smem()] * small + [vmem()] * n_in,
        out_specs=vmem() if one else tuple(vmem() for _ in outs),
        scratch_shapes=scratch,
        compiler_params=pltpu.CompilerParams(vmem_limit_bytes=VMEM_LIMIT),
        name=name,
    )


def exchange(messages, first):
    n_z = messages.shape[0]
    return lax.all_to_all(
        messages, "z", split_axis=0, concat_axis=0, axis_index_groups=[[k ^ first for k in range(n_z)]], tiled=True
    )


def per_device(queries, neighbours, key_weight, value_weight, counts, slot_map, d_attended):
    n_z, n_x, n_y, n_core = (lax.axis_size(a) for a in ("z", "x", "y", "core"))
    n_seq = n_z * n_x
    chunk = neighbours.shape[3]
    enc, width = key_weight.shape
    flat = SLOTS * chunk
    blocks = -(-flat // LANES)
    rows = SLOTS * NB_LEN

    def shape(*dims):
        return jax.ShapeDtypeStruct(dims, BF)

    turned = neighbours.transpose(1, 2, 3, 0).reshape(flat, n_seq)
    core, turned = lax.optimization_barrier((lax.axis_index("core").reshape(1), turned))
    out = call(pack_kernel, shape(n_seq, blocks, LANES), 1, "pack")(turned)
    out = exchange(out.reshape(n_z, n_x * blocks, LANES), FIRST_IN)
    out = call(spread_kernel, shape(n_x, n_y, n_z, blocks, LANES), 1, "spread")(out.reshape(n_z, n_x, blocks, LANES))
    out = lax.all_to_all(out.reshape(n_x * n_y, n_z, blocks, LANES), ("x", "y"), split_axis=0, concat_axis=0, tiled=True)
    out = call(turn_kernel, shape(n_y, flat, NB_LEN), 1, "turn")(out.reshape(n_x, n_y, n_z, blocks, LANES))
    out = lax.all_gather(out, "core", axis=0).reshape(n_core, n_y, SLOTS, chunk, NB_LEN)
    half = shape(n_y, SLOTS, chunk, NB_LEN)
    attended, d_queries, keep, send = call(
        attend_kernel,
        (shape(*queries.shape), shape(*queries.shape), half, half),
        5,
        "attend",
        small=3,
        scratch=(
            pltpu.VMEM((enc, rows), BF),
            pltpu.VMEM((width, rows), BF),
            pltpu.VMEM((width, rows), BF),
            pltpu.VMEM((n_core * n_y, chunk, rows), BF),
        ),
    )(counts, slot_map, core, out, key_weight, value_weight, queries, d_attended)
    got = lax.ppermute(send, "core", [(0, 1), (1, 0)])
    back = call(join_kernel, shape(n_x, n_y, n_z, blocks, LANES), 2, "join")(keep.reshape(n_y, flat, NB_LEN), got.reshape(n_y, flat, NB_LEN))
    back = lax.all_to_all(back.reshape(n_x * n_y, n_z, blocks, LANES), ("x", "y"), split_axis=0, concat_axis=0, tiled=True)
    back = call(sum_kernel, shape(n_z, n_x, blocks, LANES), 1, "sum")(back.reshape(n_x, n_y, n_z, blocks, LANES))
    home = exchange(back.reshape(n_z, n_x * blocks, LANES), FIRST_OUT)
    grad = call(unpack_kernel, shape(flat, n_seq), 1, "unpack")(home.reshape(n_seq, blocks, LANES))
    d_neighbours = grad.reshape(1, SLOTS, chunk, n_seq).transpose(3, 0, 1, 2)
    return (attended, d_queries, d_neighbours)


def solution(mesh):
    n_seq, n_head = mesh.devices.shape
    fine = Mesh(mesh.devices.reshape(n_seq // X_CHIPS, X_CHIPS, n_head // CORES, CORES), ("z", "x", "y", "core"))
    seq, head = ("z", "x"), ("y", "core")
    in_specs = (
        P(seq, head),
        P(None, seq, None, head),
        P(None, head),
        P(None, head),
        P(seq),
        P(seq, None),
        P(seq, head),
    )
    out_specs = (P(seq, head), P(seq, head), P(None, seq, None, head))
    return jax.shard_map(
        per_device, mesh=fine, in_specs=in_specs, out_specs=out_specs, check_vma=False
    )
```

```python
import jax
import jax.numpy as jnp
from jax import lax
from jax.experimental import pallas as pl
from jax.experimental.pallas import tpu as pltpu
from jax.sharding import Mesh, PartitionSpec as P

HDIM = 128
SPAN = 64
NB_LEN = 128
MAX_NB = 4
CH_DEV = 2
SLOTS = 8
X_CHIPS = 4
CORES = 2
FIRST_IN = 24
FIRST_OUT = 16
BF = jnp.bfloat16
F32 = jnp.float32
VMEM_LIMIT = 48 * 1024 * 1024


def vmem():
    return pl.BlockSpec(memory_space=pltpu.VMEM)


def smem():
    return pl.BlockSpec(memory_space=pltpu.SMEM)


def one_hot(n_z, n_x, first):
    n = n_z * n_x
    row = lax.broadcasted_iota(jnp.int32, (n, n), 0)
    col = lax.broadcasted_iota(jnp.int32, (n, n), 1)
    place, x = lax.rem(row, n_z), lax.div(row, n_z)
    return jnp.where(col == (place ^ first) * n_x + x, 1.0, 0.0).astype(BF)


def put_pairs(out_ref, rows):
    for i in range(out_ref.shape[1]):
        out_ref[:, i, :] = jnp.concatenate([rows[2 * i], rows[2 * i + 1]], axis=1)


def get_pairs(in_ref):
    flat = in_ref.shape[2] // 2
    return [in_ref[:, x // 2, (x % 2) * flat : (x % 2 + 1) * flat] for x in range(2 * in_ref.shape[1])]


def fold(rows):
    half = rows.shape[0] // 2
    return jnp.concatenate([rows[:half], rows[half:]], axis=1)


def unfold(rows):
    flat = rows.shape[1] // 2
    return jnp.concatenate([rows[:, :flat], rows[:, flat:]], axis=0)


def pack_kernel(flat_ref, out_ref):
    n_z, n_x = out_ref.shape[0], 2 * out_ref.shape[1]
    nt = (((1,), (1,)), ((), ()))
    turned = lax.dot_general(one_hot(n_z, n_x, FIRST_IN), flat_ref[...], nt, preferred_element_type=F32).astype(BF)
    put_pairs(out_ref, [turned[x * n_z : (x + 1) * n_z] for x in range(n_x)])


def unpack_kernel(in_ref, out_ref):
    n_z, n_x = in_ref.shape[0], 2 * in_ref.shape[1]
    rows = jnp.concatenate(get_pairs(in_ref), axis=0)
    tn = (((0,), (0,)), ((), ()))
    out_ref[...] = lax.dot_general(rows, one_hot(n_z, n_x, FIRST_OUT), tn, preferred_element_type=F32).astype(BF)


def spread_kernel(in_ref, out_ref):
    for x, rows in enumerate(get_pairs(in_ref)):
        own = fold(rows)
        for y in range(out_ref.shape[1]):
            out_ref[x, y] = own


def turn_kernel(in_ref, out_ref):
    n_x, n_y = in_ref.shape[:2]
    for y in range(n_y):
        out_ref[y] = jnp.concatenate([unfold(in_ref[x, y]) for x in range(n_x)], axis=0).T


def join_kernel(core_ref, keep_ref, both_ref, out_ref):
    n_x, n_y = out_ref.shape[:2]
    n_z = 2 * out_ref.shape[2]
    other = 1 - core_ref[0]
    for y in range(n_y):
        turned = (keep_ref[y].astype(F32) + both_ref[other, y].astype(F32)).astype(BF).T
        for x in range(n_x):
            out_ref[x, y] = fold(turned[x * n_z : (x + 1) * n_z])


def sum_kernel(in_ref, out_ref):
    n_x, n_y = in_ref.shape[:2]
    first = FIRST_IN ^ FIRST_OUT
    run = first & -first if first else out_ref.shape[0]
    rows = []
    for x in range(n_x):
        total = in_ref[x, 0].astype(F32)
        for y in range(1, n_y):
            total = total + in_ref[x, y].astype(F32)
        total = unfold(total.astype(BF))
        rows.append(jnp.concatenate([total[k ^ first : (k ^ first) + run] for k in range(0, total.shape[0], run)], axis=0))
    put_pairs(out_ref, rows)


def attend_kernel(
    counts_ref, slots_ref, core_ref, rows_ref, wk_ref, wv_ref, q_ref, g_ref, att_ref, dq_ref, keep_ref, send_ref, x_ref, dk_ref, dv_ref, part_ref
):
    n_core, n_y, _, chunk, _ = rows_ref.shape
    heads = q_ref.shape[1] // HDIM
    span_rows = MAX_NB * NB_LEN
    factor = 1.0 / HDIM**0.5
    for j in range(SLOTS):
        slot = slots_ref[0, j]
        for b in range(n_core * n_y):
            x_ref[b * chunk : (b + 1) * chunk, j * NB_LEN : (j + 1) * NB_LEN] = rows_ref[b % n_core, b // n_core, slot]
    col = lax.broadcasted_iota(jnp.int32, (1, span_rows), 1)
    bias = [jnp.where(col < counts_ref[c] * NB_LEN, 0.0, -jnp.inf) for c in range(CH_DEV)]
    nt = (((1,), (1,)), ((), ()))
    tn = (((0,), (0,)), ((), ()))
    toks = [slice(c * SPAN, (c + 1) * SPAN) for c in range(CH_DEV)]
    owns = [slice(c * span_rows, (c + 1) * span_rows) for c in range(CH_DEV)]

    def project(h):
        cols = slice(h * HDIM, (h + 1) * HDIM)
        key = lax.dot_general(wk_ref[:, cols], x_ref[...], tn, preferred_element_type=F32)
        value = lax.dot_general(wv_ref[:, cols], x_ref[...], tn, preferred_element_type=F32).astype(BF)
        key_hi = key.astype(BF)
        key_lo = (key - key_hi.astype(F32)).astype(BF)
        return jnp.concatenate([key_hi, key_lo], axis=0), value

    def score(h, c, key_two, value):
        cols = slice(h * HDIM, (h + 1) * HDIM)
        query = q_ref[toks[c], cols]
        scores = jnp.dot(jnp.concatenate([query, query], axis=1), key_two[:, owns[c]], preferred_element_type=F32)
        dprobs = jnp.dot(g_ref[toks[c], cols], value[:, owns[c]], preferred_element_type=F32)
        return scores, dprobs

    def soften(c, scores, dprobs):
        scores = scores * factor + bias[c]
        top = jnp.max(scores, axis=1, keepdims=True)
        expo = jnp.exp(scores - top)
        probs = expo * (1.0 / jnp.sum(expo, axis=1, keepdims=True))
        inner = jnp.sum(probs * dprobs, axis=1, keepdims=True)
        return probs.astype(BF), (probs * (dprobs - inner)).astype(BF)

    def finish(h, c, key_two, value, probs_b, dscores):
        cols = slice(h * HDIM, (h + 1) * HDIM)
        query, grad = q_ref[toks[c], cols], g_ref[toks[c], cols]
        att = lax.dot_general(probs_b, value[:, owns[c]], nt, preferred_element_type=F32)
        att_ref[toks[c], cols] = att.astype(BF)
        dq = lax.dot_general(dscores, key_two[:, owns[c]], nt, preferred_element_type=F32)
        dq_ref[toks[c], cols] = ((dq[:, :HDIM] + dq[:, HDIM:]) * factor).astype(BF)
        dk_ref[cols, owns[c]] = (lax.dot_general(query, dscores, tn, preferred_element_type=F32) * factor).astype(BF)
        dv_ref[cols, owns[c]] = lax.dot_general(grad, probs_b, tn, preferred_element_type=F32).astype(BF)

    pairs = [(h, c) for h in range(heads) for c in range(CH_DEV)]
    kv, raw, soft = {0: project(0)}, {}, {}
    for i in range(len(pairs) + 2):
        if i < len(pairs):
            h, c = pairs[i]
            raw[i] = score(h, c, *kv[h])
        if c == 0 and i < len(pairs) and h + 1 < heads:
            kv[h + 1] = project(h + 1)
        if 1 <= i <= len(pairs):
            soft[i - 1] = soften(pairs[i - 1][1], *raw.pop(i - 1))
        if i >= 2:
            ph, pc = pairs[i - 2]
            finish(ph, pc, *kv[ph], *soft.pop(i - 2))
    part = jnp.dot(wk_ref[...], dk_ref[...], preferred_element_type=F32)
    part = (part + jnp.dot(wv_ref[...], dv_ref[...], preferred_element_type=F32)).astype(BF)
    for b in range(n_core * n_y):
        part_ref[b] = part[b * chunk : (b + 1) * chunk]
    core = core_ref[0]
    for j in range(SLOTS):
        slot = slots_ref[0, j]
        for y in range(n_y):
            keep_ref[y, slot] = part_ref[y * n_core + core, :, j * NB_LEN : (j + 1) * NB_LEN]
            send_ref[y, slot] = part_ref[y * n_core + 1 - core, :, j * NB_LEN : (j + 1) * NB_LEN]


def call(kernel, outs, n_in, name, small=0, scratch=()):
    one = isinstance(outs, jax.ShapeDtypeStruct)
    return pl.pallas_call(
        kernel,
        out_shape=outs,
        in_specs=[smem()] * small + [vmem()] * n_in,
        out_specs=vmem() if one else tuple(vmem() for _ in outs),
        scratch_shapes=scratch,
        compiler_params=pltpu.CompilerParams(vmem_limit_bytes=VMEM_LIMIT),
        name=name,
    )


def exchange(messages, first):
    n_z = messages.shape[0]
    return lax.all_to_all(
        messages, "z", split_axis=0, concat_axis=0, axis_index_groups=[[k ^ first for k in range(n_z)]], tiled=True
    )


def per_device(queries, neighbours, key_weight, value_weight, counts, slot_map, d_attended):
    n_z, n_x, n_y, n_core = (lax.axis_size(a) for a in ("z", "x", "y", "core"))
    n_seq = n_z * n_x
    chunk = neighbours.shape[3]
    enc, width = key_weight.shape
    flat = SLOTS * chunk
    rows = SLOTS * NB_LEN

    def shape(*dims):
        return jax.ShapeDtypeStruct(dims, BF)

    pairs = shape(n_z, n_x // 2, 2 * flat)
    folded = shape(n_x, n_y, n_z // 2, 2 * flat)
    merged = (n_x * n_y, n_z // 2, 2 * flat)
    turned = neighbours.transpose(1, 2, 3, 0).reshape(flat, n_seq)
    core, turned = lax.optimization_barrier((lax.axis_index("core").reshape(1), turned))
    out = call(pack_kernel, pairs, 1, "pack")(turned)
    out = exchange(out, FIRST_IN)
    out = call(spread_kernel, folded, 1, "spread")(out)
    out = lax.all_to_all(out.reshape(merged), ("x", "y"), split_axis=0, concat_axis=0, tiled=True)
    out = call(turn_kernel, shape(n_y, flat, NB_LEN), 1, "turn")(out.reshape(folded.shape))
    out = lax.all_gather(out, "core", axis=0).reshape(n_core, n_y, SLOTS, chunk, NB_LEN)
    half = shape(n_y, SLOTS, chunk, NB_LEN)
    attended, d_queries, keep, send = call(
        attend_kernel,
        (shape(*queries.shape), shape(*queries.shape), half, half),
        5,
        "attend",
        small=3,
        scratch=(
            pltpu.VMEM((enc, rows), BF),
            pltpu.VMEM((width, rows), BF),
            pltpu.VMEM((width, rows), BF),
            pltpu.VMEM((n_core * n_y, chunk, rows), BF),
        ),
    )(counts, slot_map, core, out, key_weight, value_weight, queries, d_attended)
    both = lax.all_gather(send.reshape(n_y, flat, NB_LEN), "core", axis=0)
    back = call(join_kernel, folded, 2, "join", small=1)(core, keep.reshape(n_y, flat, NB_LEN), both)
    back = lax.all_to_all(back.reshape(merged), ("x", "y"), split_axis=0, concat_axis=0, tiled=True)
    back = call(sum_kernel, pairs, 1, "sum")(back.reshape(folded.shape))
    home = exchange(back, FIRST_OUT)
    grad = call(unpack_kernel, shape(flat, n_seq), 1, "unpack")(home)
    d_neighbours = grad.reshape(1, SLOTS, chunk, n_seq).transpose(3, 0, 1, 2)
    return (attended, d_queries, d_neighbours)


def solution(mesh):
    n_seq, n_head = mesh.devices.shape
    fine = Mesh(mesh.devices.reshape(n_seq // X_CHIPS, X_CHIPS, n_head // CORES, CORES), ("z", "x", "y", "core"))
    seq, head = ("z", "x"), ("y", "core")
    in_specs = (
        P(seq, head),
        P(None, seq, None, head),
        P(None, head),
        P(None, head),
        P(seq),
        P(seq, None),
        P(seq, head),
    )
    out_specs = (P(seq, head), P(seq, head), P(None, seq, None, head))
    return jax.shard_map(
        per_device, mesh=fine, in_specs=in_specs, out_specs=out_specs, check_vma=False
    )
```

```python
import jax
import jax.numpy as jnp
from jax import lax
from jax.experimental import pallas as pl
from jax.experimental.pallas import tpu as pltpu
from jax.sharding import Mesh, PartitionSpec as P

HDIM = 128
SPAN = 64
NB_LEN = 128
MAX_NB = 4
CH_DEV = 2
SLOTS = 8
X_CHIPS = 4
CORES = 2
FIRST_IN = 24
FIRST_OUT = 16
FIRST_X = 2
FIRST_Y = 2
BF = jnp.bfloat16
F32 = jnp.float32
VMEM_LIMIT = 48 * 1024 * 1024


def vmem():
    return pl.BlockSpec(memory_space=pltpu.VMEM)


def smem():
    return pl.BlockSpec(memory_space=pltpu.SMEM)


def one_hot(n_z, n_x, first):
    n = n_z * n_x
    row = lax.broadcasted_iota(jnp.int32, (n, n), 0)
    col = lax.broadcasted_iota(jnp.int32, (n, n), 1)
    place, x = lax.rem(row, n_z), lax.div(row, n_z)
    return jnp.where(col == (place ^ first) * n_x + x, 1.0, 0.0).astype(BF)


def put_pairs(out_ref, rows):
    for i in range(out_ref.shape[1]):
        out_ref[:, i, :] = jnp.concatenate([rows[2 * i], rows[2 * i + 1]], axis=1)


def get_pairs(in_ref):
    flat = in_ref.shape[2] // 2
    return [in_ref[:, x // 2, (x % 2) * flat : (x % 2 + 1) * flat] for x in range(2 * in_ref.shape[1])]


def fold(rows):
    half = rows.shape[0] // 2
    return jnp.concatenate([rows[:half], rows[half:]], axis=1)


def unfold(rows):
    flat = rows.shape[1] // 2
    return jnp.concatenate([rows[:, :flat], rows[:, flat:]], axis=0)


def pack_kernel(flat_ref, out_ref):
    n_z, n_x = out_ref.shape[0], 2 * out_ref.shape[1]
    nt = (((1,), (1,)), ((), ()))
    turned = lax.dot_general(one_hot(n_z, n_x, FIRST_IN), flat_ref[...], nt, preferred_element_type=F32).astype(BF)
    put_pairs(out_ref, [turned[x * n_z : (x + 1) * n_z] for x in range(n_x)])


def unpack_kernel(in_ref, att_ref, dq_ref, out_ref, att_out, dq_out, sem):
    copies = [pltpu.make_async_copy(att_ref, att_out, sem.at[0]), pltpu.make_async_copy(dq_ref, dq_out, sem.at[1])]
    for copy in copies:
        copy.start()
    n_z, n_x = in_ref.shape[0], 2 * in_ref.shape[1]
    rows = jnp.concatenate(get_pairs(in_ref), axis=0)
    tn = (((0,), (0,)), ((), ()))
    out_ref[...] = lax.dot_general(rows, one_hot(n_z, n_x, FIRST_OUT), tn, preferred_element_type=F32).astype(BF)
    for copy in copies:
        copy.wait()


def spread_kernel(in_ref, out_ref):
    for x, rows in enumerate(get_pairs(in_ref)):
        own = fold(rows)
        for y in range(out_ref.shape[1]):
            out_ref[x ^ FIRST_X, y] = own


def turn_kernel(in_ref, out_ref):
    n_x, n_y = in_ref.shape[:2]
    for y in range(n_y):
        out_ref[y ^ FIRST_Y] = jnp.concatenate([unfold(in_ref[x, y]) for x in range(n_x)], axis=0).T


def join_kernel(core_ref, keep_ref, both_ref, out_ref):
    n_x, n_y = out_ref.shape[:2]
    n_z = 2 * out_ref.shape[2]
    other = 1 - core_ref[0]
    for y in range(n_y):
        turned = (keep_ref[y].astype(F32) + both_ref[other, y].astype(F32)).astype(BF).T
        for x in range(n_x):
            out_ref[x, y ^ FIRST_Y] = fold(turned[x * n_z : (x + 1) * n_z])


def sum_kernel(in_ref, out_ref):
    n_x, n_y = in_ref.shape[:2]
    first = FIRST_IN ^ FIRST_OUT
    run = first & -first if first else out_ref.shape[0]
    rows = []
    for x in range(n_x):
        total = in_ref[x ^ FIRST_X, 0].astype(F32)
        for y in range(1, n_y):
            total = total + in_ref[x ^ FIRST_X, y].astype(F32)
        total = unfold(total.astype(BF))
        rows.append(jnp.concatenate([total[k ^ first : (k ^ first) + run] for k in range(0, total.shape[0], run)], axis=0))
    put_pairs(out_ref, rows)


def attend_kernel(
    counts_ref, slots_ref, core_ref, rows_ref, wk_ref, wv_ref, q_ref, g_ref, att_ref, dq_ref, keep_ref, send_ref, x_ref, dk_ref, dv_ref, part_ref
):
    n_core, n_y, _, chunk, _ = rows_ref.shape
    heads = q_ref.shape[1] // HDIM
    span_rows = MAX_NB * NB_LEN
    factor = 1.0 / HDIM**0.5
    for j in range(SLOTS):
        slot = slots_ref[0, j]
        for b in range(n_core * n_y):
            x_ref[b * chunk : (b + 1) * chunk, j * NB_LEN : (j + 1) * NB_LEN] = rows_ref[b % n_core, b // n_core, slot]
    col = lax.broadcasted_iota(jnp.int32, (1, span_rows), 1)
    bias = [jnp.where(col < counts_ref[c] * NB_LEN, 0.0, -jnp.inf) for c in range(CH_DEV)]
    nt = (((1,), (1,)), ((), ()))
    tn = (((0,), (0,)), ((), ()))
    toks = [slice(c * SPAN, (c + 1) * SPAN) for c in range(CH_DEV)]
    owns = [slice(c * span_rows, (c + 1) * span_rows) for c in range(CH_DEV)]

    def project(h):
        cols = slice(h * HDIM, (h + 1) * HDIM)
        key = lax.dot_general(wk_ref[:, cols], x_ref[...], tn, preferred_element_type=F32)
        value = lax.dot_general(wv_ref[:, cols], x_ref[...], tn, preferred_element_type=F32).astype(BF)
        key_hi = key.astype(BF)
        key_lo = (key - key_hi.astype(F32)).astype(BF)
        return jnp.concatenate([key_hi, key_lo], axis=0), value

    def score(h, c, key_two, value):
        cols = slice(h * HDIM, (h + 1) * HDIM)
        query = q_ref[toks[c], cols]
        scores = jnp.dot(jnp.concatenate([query, query], axis=1), key_two[:, owns[c]], preferred_element_type=F32)
        dprobs = jnp.dot(g_ref[toks[c], cols], value[:, owns[c]], preferred_element_type=F32)
        return scores, dprobs

    def soften(c, scores, dprobs):
        scores = scores * factor + bias[c]
        top = jnp.max(scores, axis=1, keepdims=True)
        expo = jnp.exp(scores - top)
        probs = expo * (1.0 / jnp.sum(expo, axis=1, keepdims=True))
        inner = jnp.sum(probs * dprobs, axis=1, keepdims=True)
        return probs.astype(BF), (probs * (dprobs - inner)).astype(BF)

    def finish(h, c, key_two, value, probs_b, dscores):
        cols = slice(h * HDIM, (h + 1) * HDIM)
        query, grad = q_ref[toks[c], cols], g_ref[toks[c], cols]
        att = lax.dot_general(probs_b, value[:, owns[c]], nt, preferred_element_type=F32)
        att_ref[toks[c], cols] = att.astype(BF)
        dq = lax.dot_general(dscores, key_two[:, owns[c]], nt, preferred_element_type=F32)
        dq_ref[toks[c], cols] = ((dq[:, :HDIM] + dq[:, HDIM:]) * factor).astype(BF)
        dk_ref[cols, owns[c]] = (lax.dot_general(query, dscores, tn, preferred_element_type=F32) * factor).astype(BF)
        dv_ref[cols, owns[c]] = lax.dot_general(grad, probs_b, tn, preferred_element_type=F32).astype(BF)

    pairs = [(h, c) for h in range(heads) for c in range(CH_DEV)]
    kv, raw, soft = {0: project(0)}, {}, {}
    for i in range(len(pairs) + 2):
        if i < len(pairs):
            h, c = pairs[i]
            raw[i] = score(h, c, *kv[h])
        if c == 0 and i < len(pairs) and h + 1 < heads:
            kv[h + 1] = project(h + 1)
        if 1 <= i <= len(pairs):
            soft[i - 1] = soften(pairs[i - 1][1], *raw.pop(i - 1))
        if i >= 2:
            ph, pc = pairs[i - 2]
            finish(ph, pc, *kv[ph], *soft.pop(i - 2))
    part = jnp.dot(wk_ref[...], dk_ref[...], preferred_element_type=F32)
    part = (part + jnp.dot(wv_ref[...], dv_ref[...], preferred_element_type=F32)).astype(BF)
    for b in range(n_core * n_y):
        part_ref[b] = part[b * chunk : (b + 1) * chunk]
    core = core_ref[0]
    for j in range(SLOTS):
        slot = slots_ref[0, j]
        for y in range(n_y):
            keep_ref[y, slot] = part_ref[y * n_core + core, :, j * NB_LEN : (j + 1) * NB_LEN]
            send_ref[y, slot] = part_ref[y * n_core + 1 - core, :, j * NB_LEN : (j + 1) * NB_LEN]


def call(kernel, outs, n_in, name, small=0, scratch=(), left=0):
    one = isinstance(outs, jax.ShapeDtypeStruct)
    return pl.pallas_call(
        kernel,
        out_shape=outs,
        in_specs=[smem()] * small + [vmem()] * n_in,
        out_specs=vmem() if one else (vmem(),) * (len(outs) - left) + (pl.BlockSpec(memory_space=pl.ANY),) * left,
        scratch_shapes=scratch,
        compiler_params=pltpu.CompilerParams(vmem_limit_bytes=VMEM_LIMIT),
        name=name,
    )


def exchange(messages, first):
    n_z = messages.shape[0]
    return lax.all_to_all(
        messages, "z", split_axis=0, concat_axis=0, axis_index_groups=[[k ^ first for k in range(n_z)]], tiled=True
    )


def exchange_xy(messages, n_y):
    first = FIRST_X * n_y + FIRST_Y
    places = [[k ^ first for k in range(messages.shape[0])]]
    return lax.all_to_all(messages, ("x", "y"), split_axis=0, concat_axis=0, axis_index_groups=places, tiled=True)


def per_device(queries, neighbours, key_weight, value_weight, counts, slot_map, d_attended):
    n_z, n_x, n_y, n_core = (lax.axis_size(a) for a in ("z", "x", "y", "core"))
    n_seq = n_z * n_x
    chunk = neighbours.shape[3]
    enc, width = key_weight.shape
    flat = SLOTS * chunk
    rows = SLOTS * NB_LEN

    def shape(*dims):
        return jax.ShapeDtypeStruct(dims, BF)

    pairs = shape(n_z, n_x // 2, 2 * flat)
    folded = shape(n_x, n_y, n_z // 2, 2 * flat)
    merged = (n_x * n_y, n_z // 2, 2 * flat)
    turned = neighbours.transpose(1, 2, 3, 0).reshape(flat, n_seq)
    core, turned = lax.optimization_barrier((lax.axis_index("core").reshape(1), turned))
    out = call(pack_kernel, pairs, 1, "pack")(turned)
    out = exchange(out, FIRST_IN)
    out = call(spread_kernel, folded, 1, "spread")(out)
    out = exchange_xy(out.reshape(merged), n_y)
    out = call(turn_kernel, shape(n_y, flat, NB_LEN), 1, "turn")(out.reshape(folded.shape))
    out = lax.all_gather(out, "core", axis=0).reshape(n_core, n_y, SLOTS, chunk, NB_LEN)
    half = shape(n_y, SLOTS, chunk, NB_LEN)
    attended, d_queries, keep, send = call(
        attend_kernel,
        (shape(*queries.shape), shape(*queries.shape), half, half),
        5,
        "attend",
        small=3,
        scratch=(
            pltpu.VMEM((enc, rows), BF),
            pltpu.VMEM((width, rows), BF),
            pltpu.VMEM((width, rows), BF),
            pltpu.VMEM((n_core * n_y, chunk, rows), BF),
        ),
    )(counts, slot_map, core, out, key_weight, value_weight, queries, d_attended)
    both = lax.all_gather(send.reshape(n_y, flat, NB_LEN), "core", axis=0)
    back = call(join_kernel, folded, 2, "join", small=1)(core, keep.reshape(n_y, flat, NB_LEN), both)
    back = exchange_xy(back.reshape(merged), n_y)
    back = call(sum_kernel, pairs, 1, "sum")(back.reshape(folded.shape))
    home = exchange(back, FIRST_OUT)
    grad, attended, d_queries = call(
        unpack_kernel,
        (shape(flat, n_seq), shape(*queries.shape), shape(*queries.shape)),
        3,
        "unpack",
        scratch=(pltpu.SemaphoreType.DMA((2,)),),
        left=2,
    )(home, attended, d_queries)
    d_neighbours = grad.reshape(1, SLOTS, chunk, n_seq).transpose(3, 0, 1, 2)
    return (attended, d_queries, d_neighbours)


def solution(mesh):
    n_seq, n_head = mesh.devices.shape
    fine = Mesh(mesh.devices.reshape(n_seq // X_CHIPS, X_CHIPS, n_head // CORES, CORES), ("z", "x", "y", "core"))
    seq, head = ("z", "x"), ("y", "core")
    in_specs = (
        P(seq, head),
        P(None, seq, None, head),
        P(None, head),
        P(None, head),
        P(seq),
        P(seq, None),
        P(seq, head),
    )
    out_specs = (P(seq, head), P(seq, head), P(None, seq, None, head))
    return jax.shard_map(
        per_device, mesh=fine, in_specs=in_specs, out_specs=out_specs, check_vma=False
    )
```

```python
import jax
import jax.numpy as jnp
from jax import lax
from jax.experimental import pallas as pl
from jax.experimental.pallas import tpu as pltpu
from jax.sharding import Mesh, PartitionSpec as P

HDIM = 128
SPAN = 64
NB_LEN = 128
MAX_NB = 4
CH_DEV = 2
SLOTS = 8
X_CHIPS = 4
CORES = 2
FIRST_IN = 20
FIRST_OUT = 16
FIRST_X = 2
FIRST_Y = 2
BF = jnp.bfloat16
F32 = jnp.float32
VMEM_LIMIT = 48 * 1024 * 1024


def vmem():
    return pl.BlockSpec(memory_space=pltpu.VMEM)


def smem():
    return pl.BlockSpec(memory_space=pltpu.SMEM)


def one_hot(n_z, n_x, first):
    n = n_z * n_x
    row = lax.broadcasted_iota(jnp.int32, (n, n), 0)
    col = lax.broadcasted_iota(jnp.int32, (n, n), 1)
    place, x = lax.rem(row, n_z), lax.div(row, n_z)
    return jnp.where(col == (place ^ first) * n_x + x, 1.0, 0.0).astype(BF)


def put_pairs(out_ref, rows):
    for i in range(out_ref.shape[1]):
        out_ref[:, i, :] = jnp.concatenate([rows[2 * i], rows[2 * i + 1]], axis=1)


def get_pairs(in_ref):
    flat = in_ref.shape[2] // 2
    return [in_ref[:, x // 2, (x % 2) * flat : (x % 2 + 1) * flat] for x in range(2 * in_ref.shape[1])]


def fold(rows):
    half = rows.shape[0] // 2
    return jnp.concatenate([rows[:half], rows[half:]], axis=1)


def unfold(rows):
    flat = rows.shape[1] // 2
    return jnp.concatenate([rows[:, :flat], rows[:, flat:]], axis=0)


def pack_kernel(flat_ref, out_ref):
    n_z, n_x = out_ref.shape[0], 2 * out_ref.shape[1]
    nt = (((1,), (1,)), ((), ()))
    turned = lax.dot_general(one_hot(n_z, n_x, FIRST_IN), flat_ref[...], nt, preferred_element_type=F32).astype(BF)
    put_pairs(out_ref, [turned[x * n_z : (x + 1) * n_z] for x in range(n_x)])


def unpack_kernel(in_ref, att_ref, dq_ref, out_ref, att_out, dq_out, sem):
    copies = [pltpu.make_async_copy(att_ref, att_out, sem.at[0]), pltpu.make_async_copy(dq_ref, dq_out, sem.at[1])]
    for copy in copies:
        copy.start()
    n_z, n_x = in_ref.shape[0], 2 * in_ref.shape[1]
    rows = jnp.concatenate(get_pairs(in_ref), axis=0)
    tn = (((0,), (0,)), ((), ()))
    out_ref[...] = lax.dot_general(rows, one_hot(n_z, n_x, FIRST_OUT), tn, preferred_element_type=F32).astype(BF)
    for copy in copies:
        copy.wait()


def spread_kernel(in_ref, out_ref):
    for x, rows in enumerate(get_pairs(in_ref)):
        own = fold(rows)
        for y in range(out_ref.shape[1]):
            out_ref[x ^ FIRST_X, y] = own


def turn_kernel(in_ref, out_ref):
    n_x, n_y = in_ref.shape[:2]
    for y in range(n_y):
        out_ref[y ^ FIRST_Y] = jnp.concatenate([unfold(in_ref[x, y]) for x in range(n_x)], axis=0).T


def join_kernel(core_ref, keep_ref, both_ref, out_ref):
    n_x, n_y = out_ref.shape[:2]
    n_z = 2 * out_ref.shape[2]
    other = 1 - core_ref[0]
    for y in range(n_y):
        turned = (keep_ref[y].astype(F32) + both_ref[other, y].astype(F32)).astype(BF).T
        for x in range(n_x):
            out_ref[x, y ^ FIRST_Y] = fold(turned[x * n_z : (x + 1) * n_z])


def sum_kernel(in_ref, out_ref):
    n_x, n_y = in_ref.shape[:2]
    first = FIRST_IN ^ FIRST_OUT
    run = first & -first if first else out_ref.shape[0]
    rows = []
    for x in range(n_x):
        total = in_ref[x ^ FIRST_X, 0].astype(F32)
        for y in range(1, n_y):
            total = total + in_ref[x ^ FIRST_X, y].astype(F32)
        total = unfold(total.astype(BF))
        rows.append(jnp.concatenate([total[k ^ first : (k ^ first) + run] for k in range(0, total.shape[0], run)], axis=0))
    put_pairs(out_ref, rows)


def attend_kernel(
    counts_ref, slots_ref, core_ref, rows_ref, wk_ref, wv_ref, q_ref, g_ref, att_ref, dq_ref, keep_ref, send_ref, x_ref, dk_ref, dv_ref, part_ref
):
    n_core, n_y, _, chunk, _ = rows_ref.shape
    heads = q_ref.shape[1] // HDIM
    span_rows = MAX_NB * NB_LEN
    factor = 1.0 / HDIM**0.5
    for j in range(SLOTS):
        slot = slots_ref[0, j]
        for b in range(n_core * n_y):
            x_ref[b * chunk : (b + 1) * chunk, j * NB_LEN : (j + 1) * NB_LEN] = rows_ref[b % n_core, b // n_core, slot]
    col = lax.broadcasted_iota(jnp.int32, (1, span_rows), 1)
    bias = [jnp.where(col < counts_ref[c] * NB_LEN, 0.0, -jnp.inf) for c in range(CH_DEV)]
    nt = (((1,), (1,)), ((), ()))
    tn = (((0,), (0,)), ((), ()))
    toks = [slice(c * SPAN, (c + 1) * SPAN) for c in range(CH_DEV)]
    owns = [slice(c * span_rows, (c + 1) * span_rows) for c in range(CH_DEV)]

    def project(h):
        cols = slice(h * HDIM, (h + 1) * HDIM)
        key = lax.dot_general(wk_ref[:, cols], x_ref[...], tn, preferred_element_type=F32)
        value = lax.dot_general(wv_ref[:, cols], x_ref[...], tn, preferred_element_type=F32).astype(BF)
        key_hi = key.astype(BF)
        key_lo = (key - key_hi.astype(F32)).astype(BF)
        return jnp.concatenate([key_hi, key_lo], axis=0), value

    def score(h, c, key_two, value):
        cols = slice(h * HDIM, (h + 1) * HDIM)
        query = q_ref[toks[c], cols]
        scores = jnp.dot(jnp.concatenate([query, query], axis=1), key_two[:, owns[c]], preferred_element_type=F32)
        dprobs = jnp.dot(g_ref[toks[c], cols], value[:, owns[c]], preferred_element_type=F32)
        return scores, dprobs

    def soften(c, scores, dprobs):
        scores = scores * factor + bias[c]
        top = jnp.max(scores, axis=1, keepdims=True)
        expo = jnp.exp(scores - top)
        probs = expo * (1.0 / jnp.sum(expo, axis=1, keepdims=True))
        inner = jnp.sum(probs * dprobs, axis=1, keepdims=True)
        return probs.astype(BF), (probs * (dprobs - inner)).astype(BF)

    def finish(h, c, key_two, value, probs_b, dscores):
        cols = slice(h * HDIM, (h + 1) * HDIM)
        query, grad = q_ref[toks[c], cols], g_ref[toks[c], cols]
        att = lax.dot_general(probs_b, value[:, owns[c]], nt, preferred_element_type=F32)
        att_ref[toks[c], cols] = att.astype(BF)
        dq = lax.dot_general(dscores, key_two[:, owns[c]], nt, preferred_element_type=F32)
        dq_ref[toks[c], cols] = ((dq[:, :HDIM] + dq[:, HDIM:]) * factor).astype(BF)
        dk_ref[cols, owns[c]] = (lax.dot_general(query, dscores, tn, preferred_element_type=F32) * factor).astype(BF)
        dv_ref[cols, owns[c]] = lax.dot_general(grad, probs_b, tn, preferred_element_type=F32).astype(BF)

    pairs = [(h, c) for h in range(heads) for c in range(CH_DEV)]
    kv, raw, soft = {0: project(0)}, {}, {}
    for i in range(len(pairs) + 2):
        if i < len(pairs):
            h, c = pairs[i]
            raw[i] = score(h, c, *kv[h])
        if c == 0 and i < len(pairs) and h + 1 < heads:
            kv[h + 1] = project(h + 1)
        if 1 <= i <= len(pairs):
            soft[i - 1] = soften(pairs[i - 1][1], *raw.pop(i - 1))
        if i >= 2:
            ph, pc = pairs[i - 2]
            finish(ph, pc, *kv[ph], *soft.pop(i - 2))
    part = jnp.dot(wk_ref[...], dk_ref[...], preferred_element_type=F32)
    part = (part + jnp.dot(wv_ref[...], dv_ref[...], preferred_element_type=F32)).astype(BF)
    for b in range(n_core * n_y):
        part_ref[b] = part[b * chunk : (b + 1) * chunk]
    core = core_ref[0]
    for j in range(SLOTS):
        slot = slots_ref[0, j]
        for y in range(n_y):
            keep_ref[y, slot] = part_ref[y * n_core + core, :, j * NB_LEN : (j + 1) * NB_LEN]
            send_ref[y, slot] = part_ref[y * n_core + 1 - core, :, j * NB_LEN : (j + 1) * NB_LEN]


def call(kernel, outs, n_in, name, small=0, scratch=(), left=0):
    one = isinstance(outs, jax.ShapeDtypeStruct)
    return pl.pallas_call(
        kernel,
        out_shape=outs,
        in_specs=[smem()] * small + [vmem()] * n_in,
        out_specs=vmem() if one else (vmem(),) * (len(outs) - left) + (pl.BlockSpec(memory_space=pl.ANY),) * left,
        scratch_shapes=scratch,
        compiler_params=pltpu.CompilerParams(vmem_limit_bytes=VMEM_LIMIT),
        name=name,
    )


def exchange(messages, first):
    n_z = messages.shape[0]
    return lax.all_to_all(
        messages, "z", split_axis=0, concat_axis=0, axis_index_groups=[[k ^ first for k in range(n_z)]], tiled=True
    )


def exchange_xy(messages, n_y):
    first = FIRST_X * n_y + FIRST_Y
    places = [[k ^ first for k in range(messages.shape[0])]]
    return lax.all_to_all(messages, ("x", "y"), split_axis=0, concat_axis=0, axis_index_groups=places, tiled=True)


def per_device(queries, neighbours, key_weight, value_weight, counts, slot_map, d_attended):
    n_z, n_x, n_y, n_core = (lax.axis_size(a) for a in ("z", "x", "y", "core"))
    n_seq = n_z * n_x
    chunk = neighbours.shape[3]
    enc, width = key_weight.shape
    flat = SLOTS * chunk
    rows = SLOTS * NB_LEN

    def shape(*dims):
        return jax.ShapeDtypeStruct(dims, BF)

    pairs = shape(n_z, n_x // 2, 2 * flat)
    folded = shape(n_x, n_y, n_z // 2, 2 * flat)
    merged = (n_x * n_y, n_z // 2, 2 * flat)
    turned = neighbours.transpose(1, 2, 3, 0).reshape(flat, n_seq)
    core, turned = lax.optimization_barrier((lax.axis_index("core").reshape(1), turned))
    out = call(pack_kernel, pairs, 1, "pack")(turned)
    out = exchange(out, FIRST_IN)
    out = call(spread_kernel, folded, 1, "spread")(out)
    out = exchange_xy(out.reshape(merged), n_y)
    out = call(turn_kernel, shape(n_y, flat, NB_LEN), 1, "turn")(out.reshape(folded.shape))
    out = lax.all_gather(out, "core", axis=0).reshape(n_core, n_y, SLOTS, chunk, NB_LEN)
    half = shape(n_y, SLOTS, chunk, NB_LEN)
    attended, d_queries, keep, send = call(
        attend_kernel,
        (shape(*queries.shape), shape(*queries.shape), half, half),
        5,
        "attend",
        small=3,
        scratch=(
            pltpu.VMEM((enc, rows), BF),
            pltpu.VMEM((width, rows), BF),
            pltpu.VMEM((width, rows), BF),
            pltpu.VMEM((n_core * n_y, chunk, rows), BF),
        ),
    )(counts, slot_map, core, out, key_weight, value_weight, queries, d_attended)
    both = lax.all_gather(send.reshape(n_y, flat, NB_LEN), "core", axis=0)
    back = call(join_kernel, folded, 2, "join", small=1)(core, keep.reshape(n_y, flat, NB_LEN), both)
    back = exchange_xy(back.reshape(merged), n_y)
    back = call(sum_kernel, pairs, 1, "sum")(back.reshape(folded.shape))
    home = exchange(back, FIRST_OUT)
    grad, attended, d_queries = call(
        unpack_kernel,
        (shape(flat, n_seq), shape(*queries.shape), shape(*queries.shape)),
        3,
        "unpack",
        scratch=(pltpu.SemaphoreType.DMA((2,)),),
        left=2,
    )(home, attended, d_queries)
    d_neighbours = grad.reshape(1, SLOTS, chunk, n_seq).transpose(3, 0, 1, 2)
    return (attended, d_queries, d_neighbours)


def solution(mesh):
    n_seq, n_head = mesh.devices.shape
    fine = Mesh(mesh.devices.reshape(n_seq // X_CHIPS, X_CHIPS, n_head // CORES, CORES), ("z", "x", "y", "core"))
    seq, head = ("z", "x"), ("y", "core")
    in_specs = (
        P(seq, head),
        P(None, seq, None, head),
        P(None, head),
        P(None, head),
        P(seq),
        P(seq, None),
        P(seq, head),
    )
    out_specs = (P(seq, head), P(seq, head), P(None, seq, None, head))
    return jax.shard_map(
        per_device, mesh=fine, in_specs=in_specs, out_specs=out_specs, check_vma=False
    )
```

```python
import jax
import jax.numpy as jnp
from jax import lax
from jax.experimental import pallas as pl
from jax.experimental.pallas import tpu as pltpu
from jax.sharding import Mesh, PartitionSpec as P

HDIM = 128
SPAN = 64
NB_LEN = 128
MAX_NB = 4
CH_DEV = 2
SLOTS = 8
X_CHIPS = 4
CORES = 2
FIRST_IN = 20
FIRST_OUT = 18
FIRST_X = 2
FIRST_Y = 2
BF = jnp.bfloat16
F32 = jnp.float32
VMEM_LIMIT = 48 * 1024 * 1024


def vmem():
    return pl.BlockSpec(memory_space=pltpu.VMEM)


def smem():
    return pl.BlockSpec(memory_space=pltpu.SMEM)


def one_hot(n_z, n_x, first):
    n = n_z * n_x
    row = lax.broadcasted_iota(jnp.int32, (n, n), 0)
    col = lax.broadcasted_iota(jnp.int32, (n, n), 1)
    place, x = lax.rem(row, n_z), lax.div(row, n_z)
    return jnp.where(col == (place ^ first) * n_x + x, 1.0, 0.0).astype(BF)


def put_pairs(out_ref, rows):
    for i in range(out_ref.shape[1]):
        out_ref[:, i, :] = jnp.concatenate([rows[2 * i], rows[2 * i + 1]], axis=1)


def get_pairs(in_ref):
    flat = in_ref.shape[2] // 2
    return [in_ref[:, x // 2, (x % 2) * flat : (x % 2 + 1) * flat] for x in range(2 * in_ref.shape[1])]


def fold(rows):
    half = rows.shape[0] // 2
    return jnp.concatenate([rows[:half], rows[half:]], axis=1)


def unfold(rows):
    flat = rows.shape[1] // 2
    return jnp.concatenate([rows[:, :flat], rows[:, flat:]], axis=0)


def pack_kernel(flat_ref, out_ref):
    n_z, n_x = out_ref.shape[0], 2 * out_ref.shape[1]
    nt = (((1,), (1,)), ((), ()))
    turned = lax.dot_general(one_hot(n_z, n_x, FIRST_IN), flat_ref[...], nt, preferred_element_type=F32).astype(BF)
    put_pairs(out_ref, [turned[x * n_z : (x + 1) * n_z] for x in range(n_x)])


def unpack_kernel(in_ref, att_ref, dq_ref, out_ref, att_out, dq_out, sem):
    copies = [pltpu.make_async_copy(att_ref, att_out, sem.at[0]), pltpu.make_async_copy(dq_ref, dq_out, sem.at[1])]
    for copy in copies:
        copy.start()
    n_z, n_x = in_ref.shape[0], 2 * in_ref.shape[1]
    rows = jnp.concatenate(get_pairs(in_ref), axis=0)
    tn = (((0,), (0,)), ((), ()))
    out_ref[...] = lax.dot_general(rows, one_hot(n_z, n_x, FIRST_OUT), tn, preferred_element_type=F32).astype(BF)
    for copy in copies:
        copy.wait()


def spread_kernel(in_ref, out_ref):
    for x, rows in enumerate(get_pairs(in_ref)):
        own = fold(rows)
        for y in range(out_ref.shape[1]):
            out_ref[x ^ FIRST_X, y] = own


def turn_kernel(in_ref, out_ref):
    n_x, n_y = in_ref.shape[:2]
    for y in range(n_y):
        out_ref[y ^ FIRST_Y] = jnp.concatenate([unfold(in_ref[x, y]) for x in range(n_x)], axis=0).T


def join_kernel(core_ref, keep_ref, both_ref, out_ref):
    n_x, n_y = out_ref.shape[:2]
    n_z = 2 * out_ref.shape[2]
    other = 1 - core_ref[0]
    for y in range(n_y):
        turned = (keep_ref[y].astype(F32) + both_ref[other, y].astype(F32)).astype(BF).T
        for x in range(n_x):
            out_ref[x, y ^ FIRST_Y] = fold(turned[x * n_z : (x + 1) * n_z])


def sum_kernel(in_ref, out_ref):
    n_x, n_y = in_ref.shape[:2]
    first = FIRST_IN ^ FIRST_OUT
    run = first & -first if first else out_ref.shape[0]
    rows = []
    for x in range(n_x):
        total = in_ref[x ^ FIRST_X, 0].astype(F32)
        for y in range(1, n_y):
            total = total + in_ref[x ^ FIRST_X, y].astype(F32)
        total = unfold(total.astype(BF))
        rows.append(jnp.concatenate([total[k ^ first : (k ^ first) + run] for k in range(0, total.shape[0], run)], axis=0))
    put_pairs(out_ref, rows)


def attend_kernel(
    counts_ref, slots_ref, core_ref, rows_ref, wk_ref, wv_ref, q_ref, g_ref, att_ref, dq_ref, keep_ref, send_ref, x_ref, dk_ref, dv_ref, part_ref
):
    n_core, n_y, _, chunk, _ = rows_ref.shape
    heads = q_ref.shape[1] // HDIM
    span_rows = MAX_NB * NB_LEN
    factor = 1.0 / HDIM**0.5
    for j in range(SLOTS):
        slot = slots_ref[0, j]
        for b in range(n_core * n_y):
            x_ref[b * chunk : (b + 1) * chunk, j * NB_LEN : (j + 1) * NB_LEN] = rows_ref[b % n_core, b // n_core, slot]
    col = lax.broadcasted_iota(jnp.int32, (1, span_rows), 1)
    bias = [jnp.where(col < counts_ref[c] * NB_LEN, 0.0, -jnp.inf) for c in range(CH_DEV)]
    nt = (((1,), (1,)), ((), ()))
    tn = (((0,), (0,)), ((), ()))
    toks = [slice(c * SPAN, (c + 1) * SPAN) for c in range(CH_DEV)]
    owns = [slice(c * span_rows, (c + 1) * span_rows) for c in range(CH_DEV)]

    def project(h):
        cols = slice(h * HDIM, (h + 1) * HDIM)
        key = lax.dot_general(wk_ref[:, cols], x_ref[...], tn, preferred_element_type=F32)
        value = lax.dot_general(wv_ref[:, cols], x_ref[...], tn, preferred_element_type=F32).astype(BF)
        key_hi = key.astype(BF)
        key_lo = (key - key_hi.astype(F32)).astype(BF)
        return jnp.concatenate([key_hi, key_lo], axis=0), value

    def score(h, c, key_two, value):
        cols = slice(h * HDIM, (h + 1) * HDIM)
        query = q_ref[toks[c], cols]
        scores = jnp.dot(jnp.concatenate([query, query], axis=1), key_two[:, owns[c]], preferred_element_type=F32)
        dprobs = jnp.dot(g_ref[toks[c], cols], value[:, owns[c]], preferred_element_type=F32)
        return scores, dprobs

    def soften(c, scores, dprobs):
        scores = scores * factor + bias[c]
        top = jnp.max(scores, axis=1, keepdims=True)
        expo = jnp.exp(scores - top)
        probs = expo * (1.0 / jnp.sum(expo, axis=1, keepdims=True))
        inner = jnp.sum(probs * dprobs, axis=1, keepdims=True)
        return probs.astype(BF), (probs * (dprobs - inner)).astype(BF)

    def finish(h, c, key_two, value, probs_b, dscores):
        cols = slice(h * HDIM, (h + 1) * HDIM)
        query, grad = q_ref[toks[c], cols], g_ref[toks[c], cols]
        att = lax.dot_general(probs_b, value[:, owns[c]], nt, preferred_element_type=F32)
        att_ref[toks[c], cols] = att.astype(BF)
        dq = lax.dot_general(dscores, key_two[:, owns[c]], nt, preferred_element_type=F32)
        dq_ref[toks[c], cols] = ((dq[:, :HDIM] + dq[:, HDIM:]) * factor).astype(BF)
        dk_ref[cols, owns[c]] = (lax.dot_general(query, dscores, tn, preferred_element_type=F32) * factor).astype(BF)
        dv_ref[cols, owns[c]] = lax.dot_general(grad, probs_b, tn, preferred_element_type=F32).astype(BF)

    pairs = [(h, c) for h in range(heads) for c in range(CH_DEV)]
    kv, raw, soft = {0: project(0)}, {}, {}
    for i in range(len(pairs) + 2):
        if i < len(pairs):
            h, c = pairs[i]
            raw[i] = score(h, c, *kv[h])
        if c == 0 and i < len(pairs) and h + 1 < heads:
            kv[h + 1] = project(h + 1)
        if 1 <= i <= len(pairs):
            soft[i - 1] = soften(pairs[i - 1][1], *raw.pop(i - 1))
        if i >= 2:
            ph, pc = pairs[i - 2]
            finish(ph, pc, *kv[ph], *soft.pop(i - 2))
    part = jnp.dot(wk_ref[...], dk_ref[...], preferred_element_type=F32)
    part = (part + jnp.dot(wv_ref[...], dv_ref[...], preferred_element_type=F32)).astype(BF)
    for b in range(n_core * n_y):
        part_ref[b] = part[b * chunk : (b + 1) * chunk]
    core = core_ref[0]
    for j in range(SLOTS):
        slot = slots_ref[0, j]
        for y in range(n_y):
            keep_ref[y, slot] = part_ref[y * n_core + core, :, j * NB_LEN : (j + 1) * NB_LEN]
            send_ref[y, slot] = part_ref[y * n_core + 1 - core, :, j * NB_LEN : (j + 1) * NB_LEN]


def call(kernel, outs, n_in, name, small=0, scratch=(), left=0):
    one = isinstance(outs, jax.ShapeDtypeStruct)
    return pl.pallas_call(
        kernel,
        out_shape=outs,
        in_specs=[smem()] * small + [vmem()] * n_in,
        out_specs=vmem() if one else (vmem(),) * (len(outs) - left) + (pl.BlockSpec(memory_space=pl.ANY),) * left,
        scratch_shapes=scratch,
        compiler_params=pltpu.CompilerParams(vmem_limit_bytes=VMEM_LIMIT),
        name=name,
    )


def exchange(messages, first):
    n_z = messages.shape[0]
    return lax.all_to_all(
        messages, "z", split_axis=0, concat_axis=0, axis_index_groups=[[k ^ first for k in range(n_z)]], tiled=True
    )


def exchange_xy(messages, n_y):
    first = FIRST_X * n_y + FIRST_Y
    places = [[k ^ first for k in range(messages.shape[0])]]
    return lax.all_to_all(messages, ("x", "y"), split_axis=0, concat_axis=0, axis_index_groups=places, tiled=True)


def per_device(queries, neighbours, key_weight, value_weight, counts, slot_map, d_attended):
    n_z, n_x, n_y, n_core = (lax.axis_size(a) for a in ("z", "x", "y", "core"))
    n_seq = n_z * n_x
    chunk = neighbours.shape[3]
    enc, width = key_weight.shape
    flat = SLOTS * chunk
    rows = SLOTS * NB_LEN

    def shape(*dims):
        return jax.ShapeDtypeStruct(dims, BF)

    pairs = shape(n_z, n_x // 2, 2 * flat)
    folded = shape(n_x, n_y, n_z // 2, 2 * flat)
    merged = (n_x * n_y, n_z // 2, 2 * flat)
    turned = neighbours.transpose(1, 2, 3, 0).reshape(flat, n_seq)
    core, turned = lax.optimization_barrier((lax.axis_index("core").reshape(1), turned))
    out = call(pack_kernel, pairs, 1, "pack")(turned)
    out = exchange(out, FIRST_IN)
    out = call(spread_kernel, folded, 1, "spread")(out)
    out = exchange_xy(out.reshape(merged), n_y)
    out = call(turn_kernel, shape(n_y, flat, NB_LEN), 1, "turn")(out.reshape(folded.shape))
    out = lax.all_gather(out, "core", axis=0).reshape(n_core, n_y, SLOTS, chunk, NB_LEN)
    half = shape(n_y, SLOTS, chunk, NB_LEN)
    attended, d_queries, keep, send = call(
        attend_kernel,
        (shape(*queries.shape), shape(*queries.shape), half, half),
        5,
        "attend",
        small=3,
        scratch=(
            pltpu.VMEM((enc, rows), BF),
            pltpu.VMEM((width, rows), BF),
            pltpu.VMEM((width, rows), BF),
            pltpu.VMEM((n_core * n_y, chunk, rows), BF),
        ),
    )(counts, slot_map, core, out, key_weight, value_weight, queries, d_attended)
    both = lax.all_gather(send.reshape(n_y, flat, NB_LEN), "core", axis=0)
    back = call(join_kernel, folded, 2, "join", small=1)(core, keep.reshape(n_y, flat, NB_LEN), both)
    back = exchange_xy(back.reshape(merged), n_y)
    back = call(sum_kernel, pairs, 1, "sum")(back.reshape(folded.shape))
    home = exchange(back, FIRST_OUT)
    grad, attended, d_queries = call(
        unpack_kernel,
        (shape(flat, n_seq), shape(*queries.shape), shape(*queries.shape)),
        3,
        "unpack",
        scratch=(pltpu.SemaphoreType.DMA((2,)),),
        left=2,
    )(home, attended, d_queries)
    d_neighbours = grad.reshape(1, SLOTS, chunk, n_seq).transpose(3, 0, 1, 2)
    return (attended, d_queries, d_neighbours)


def solution(mesh):
    n_seq, n_head = mesh.devices.shape
    fine = Mesh(mesh.devices.reshape(n_seq // X_CHIPS, X_CHIPS, n_head // CORES, CORES), ("z", "x", "y", "core"))
    seq, head = ("z", "x"), ("y", "core")
    in_specs = (
        P(seq, head),
        P(None, seq, None, head),
        P(None, head),
        P(None, head),
        P(seq),
        P(seq, None),
        P(seq, head),
    )
    out_specs = (P(seq, head), P(seq, head), P(None, seq, None, head))
    return jax.shard_map(
        per_device, mesh=fine, in_specs=in_specs, out_specs=out_specs, check_vma=False
    )
```
